256 devices in a mesh: row: 8 (over z_hi, core), col: 32 (over z_lo, x, y).
Axes of the slice: x: 4, y: 4, z: 8 (z_hi: 4, z_lo: 2; z = z_hi * 2 + z_lo), core: 2. Of those that a mesh axis runs over, the one named last changes fastest.
Arguments:
- panel_adj: float32 [14336, 512], P('row', 'col'), may hold values from -6 to 6
- inv_diag: float32 [512, 512], P('col'), may hold values from -0.25 to 0.25
- row_panel: float32 [512, 14336], P('row', 'col'), may hold values from -0.25 to 0.25
- trailing_adj: float32 [14336, 14336], P('row', 'col'), may hold values from -6 to 6
- trailing_factor: float32 [14336, 14336], P('row', 'col'), may hold values from -0.046875 to 0.046875
Outputs:
- trailing_new: float32 [14336, 14336], P('row', 'col')
- row_adj: float32 [512, 14336], P('row', 'col')
The draws below stay inside these ranges and needn't reach their ends.
All inputs are finite; a program needn't handle non-finite values.
Results may differ from the reference program's by a relative error of at most 0.00007.
Values sent between devices are 32-bit elements; how exact they have to be, the bound alone decides.
A program may use at most 64 MiB of HBM per device.

```python
import jax
import jax.numpy as jnp
from jax import lax

NB = 512
M = 14336


def block_scale(own_key, dims, pieces, least, high):
    def one(dim, blocks):
        heights = jax.random.uniform(jax.random.fold_in(jax.random.fold_in(own_key, 6), dim), (blocks,), jnp.float32, least / len(pieces), high / len(pieces))
        return jnp.repeat(jnp.exp(heights), dims[dim] // blocks).reshape((-1,) + (1,) * (len(dims) - dim - 1))

    factor_of = one(*pieces[0])
    for cut in pieces[1:]:
        factor_of = factor_of * one(*cut)
    return factor_of


def gaussian(key, dims, scale, reach, cuts=(), dtype=jnp.bfloat16):
    entries = jax.random.normal(key, dims, jnp.float32) * scale
    if len(cuts) > 0:
        entries = block_scale(key, dims, cuts, -0.22, 0.18) * entries
    return jnp.clip(entries, min=-reach, max=reach).astype(dtype)


def setup_inputs(seed: int = 0) -> dict:
    keys = jax.random.split(jax.random.key(seed), 6)
    panel_adj = gaussian(keys[0], (M, NB), 1.0, 6.0, ((0, 8), (1, 32)), jnp.float32)
    inv_diag = gaussian(keys[1], (NB, NB), NB ** -0.5, 0.25, ((0, 32),), jnp.float32)
    row_panel = gaussian(keys[2], (NB, M), NB ** -0.5, 0.25, ((0, 8), (1, 32)), jnp.float32)
    trailing_adj = gaussian(keys[3], (M, M), 1.0, 6.0, ((0, 8), (1, 32)), jnp.float32)
    trailing_factor = gaussian(keys[4], (M, M), M ** -0.5, 0.046875, ((0, 8), (1, 32)), jnp.float32)
    return dict(panel_adj=panel_adj, inv_diag=inv_diag, row_panel=row_panel, trailing_adj=trailing_adj, trailing_factor=trailing_factor)


def reference(panel_adj, inv_diag, row_panel, trailing_adj, trailing_factor):
    highest = lax.Precision.HIGHEST
    scaled = jnp.dot(panel_adj, inv_diag, precision=highest, preferred_element_type=jnp.float32)
    trailing_new = trailing_adj - jnp.dot(scaled, row_panel, precision=highest, preferred_element_type=jnp.float32)
    row_adj = lax.dot_general(scaled, trailing_factor, (((0,), (0,)), ((), ())), precision=highest, preferred_element_type=jnp.float32)
    return trailing_new, row_adj
```

```python
import jax
import jax.numpy as jnp
from jax import lax
from jax.experimental import pallas as pl
from jax.experimental.pallas import tpu as pltpu
from jax.sharding import PartitionSpec as P

MESH = pl.DeviceIdType.MESH
f32, bf16 = jnp.float32, jnp.bfloat16
ROWS, COLS, DEPTH, KS, HALF = 1792, 448, 512, 16, 256
WIDE = ROWS + HALF
STEPS = (0, 3, 1, 2)


def split(v):
    hi = v.astype(bf16)
    return hi, (v - hi.astype(f32)).astype(bf16)


def dot(a, b, dims):
    return lax.dot_general(a, b, (dims, ((), ())), preferred_element_type=f32)


def dot3(ah, al, bh, bl, dims):
    rows = ah.shape[0]
    both = dot(jnp.concatenate([ah, al], axis=0), bh, dims)
    return both[:rows] + both[rows:] + dot(ah, bl, dims)


def kernel(
    panel, inv, rowp, adj, fac, out, radj,
    z, fbuf, fh, fl, abuf, ph, pL, dbuf, ra, tm, tp, th, tl, wm, wp, wh, wl, us, ur,
    ssem, rsem, rs_s, rs_r, ts_s, ts_r, ws, us_s, us_r, loc, outsem,
):
    row, col = lax.axis_index("row"), lax.axis_index("col")
    h, core = row // 2, row % 2
    zl, x, y = col // 16, (col // 4) % 4, col % 4
    ia = x + core * (y - x)
    ib = y + core * (x - y)

    def device(zz, a, b):
        return (row, zz * 16 + a * (4 - 3 * core) + b * (1 + 3 * core))

    def off(i, d):
        return (i + d) % 4

    mate = device(1 - zl, ia, ib)
    ap, am = device(zl, off(ia, 1), ib), device(zl, off(ia, 3), ib)
    bp, bm = device(zl, ia, off(ib, 1)), device(zl, ia, off(ib, 3))
    partner = (2 * h + 1 - core, col)
    group = [(2 * ((h + d) % 4) + core, col) for d in (1, 2, 3)]

    def plane(dz):
        return zl if dz == 0 else 1 - zl

    own = z.at[zl, ia, ib]
    l_panel = pltpu.make_async_copy(panel, own.at[:, pl.ds(0, ROWS)], loc.at[0])
    l_inv = pltpu.make_async_copy(inv, dbuf, loc.at[1])
    l_row = pltpu.make_async_copy(rowp, ra.at[h], loc.at[2])
    l_fac = pltpu.make_async_copy(fac, fbuf, loc.at[3])
    l_adj = pltpu.make_async_copy(adj, abuf, loc.at[4])
    l_inv.start()
    l_panel.start()
    l_row.start()
    l_fac.start()
    l_adj.start()

    barrier = pltpu.get_barrier_semaphore()
    others = [mate, ap, am, bp, bm, partner] + group
    for other in others:
        pl.semaphore_signal(barrier, inc=1, device_id=other, device_id_type=MESH)
    l_inv.wait()
    d = dbuf[...]
    even = jnp.concatenate([d[:, 128 * i : 128 * i + 64] for i in range(4)], axis=1)
    odd = jnp.concatenate([d[:, 128 * i + 64 : 128 * i + 128] for i in range(4)], axis=1)
    z[zl, ia, ib, :, ROWS:WIDE] = jnp.where(core == 0, even, odd)
    l_panel.wait()
    l_row.wait()
    pl.semaphore_wait(barrier, len(others))

    sends = []

    def kind_a(dz, m):
        return 1 + dz * 4 + m

    def kind_b(dz, n, m):
        return 9 + (dz * 4 + n) * 4 + m

    def part(zz, a, b, half):
        ref = z.at[zz, a, b]
        return ref if half is None else ref.at[pl.ds(8 * half, 8)]

    def send(kind, ref, target):
        copy = pltpu.make_async_remote_copy(
            src_ref=ref, dst_ref=ref, send_sem=ssem.at[kind], recv_sem=rsem.at[kind],
            device_id=target, device_id_type=MESH,
        )
        copy.start()
        sends.append(copy)

    def arrive(kind, ref):
        pltpu.make_async_remote_copy(
            src_ref=ref, dst_ref=ref, send_sem=ssem.at[kind], recv_sem=rsem.at[kind],
            device_id=mate, device_id_type=MESH,
        ).wait_recv()

    def send_a(dz):
        ref = part(plane(dz), ia, ib, None)
        send(kind_a(dz, 0), ref, ap)
        send(kind_a(dz, 1), ref, am)

    def send_b(dz, n):
        ref = part(plane(dz), off(ia, STEPS[n]), ib, None)
        send(kind_b(dz, n, 0), ref, bp)
        send(kind_b(dz, n, 1), ref, bm)

    def relay_a(dz):
        for m, target in ((0, ap), (1, am)):
            a = off(ia, 3 if m == 0 else 1)
            arrive(kind_a(dz, m), part(plane(dz), a, ib, None))
            send(kind_a(dz, 2 + m), part(plane(dz), a, ib, m), target)
            send_b(dz, 1 + m)

    def relay_b(dz, n):
        a = off(ia, STEPS[n])
        for m, target in ((0, bp), (1, bm)):
            b = off(ib, 3 if m == 0 else 1)
            arrive(kind_b(dz, n, m), part(plane(dz), a, b, None))
            send(kind_b(dz, n, 2 + m), part(plane(dz), a, b, m), target)

    def far_a(dz):
        for m in (0, 1):
            arrive(kind_a(dz, 2 + m), part(plane(dz), off(ia, 2), ib, m))
        send_b(dz, 3)

    def far_b(dz, n):
        for m in (0, 1):
            arrive(kind_b(dz, n, 2 + m), part(plane(dz), off(ia, STEPS[n]), off(ib, 2), m))

    send(0, part(zl, ia, ib, None), mate)
    send_a(0)
    send_b(0, 0)
    r_sends = []
    for i in (1, 0, 2):
        copy = pltpu.make_async_remote_copy(
            src_ref=ra.at[h], dst_ref=ra.at[h], send_sem=rs_s.at[i], recv_sem=rs_r.at[i],
            device_id=group[i], device_id_type=MESH,
        )
        copy.start()
        r_sends.append(copy)

    l_fac.wait()
    for j in range(7):
        cut = pl.ds(256 * j, 256)
        hi, lo = split(fbuf[:, cut])
        fh[:, cut] = hi
        fl[:, cut] = lo

    t_sends = []

    def product(pieces):
        v = jnp.concatenate(
            [z[plane(dz), off(ia, STEPS[n]), :, :, 0:ROWS].reshape(64, ROWS) for dz, n in pieces], axis=0
        )
        hi, lo = split(v)
        for i, (dz, n) in enumerate(pieces):
            at = (plane(dz), off(ia, STEPS[n]))
            ph[at] = hi[64 * i : 64 * i + 64].reshape(4, 16, ROWS)
            pL[at] = lo[64 * i : 64 * i + 64].reshape(4, 16, ROWS)
        t = dot3(hi, lo, fh[...], fl[...], ((1,), (1,)))
        for i, (dz, n) in enumerate(pieces):
            at = (plane(dz), off(ia, STEPS[n]))
            tm[at] = t[64 * i : 64 * i + 64].reshape(4, 16, COLS)
        for dz, n in pieces:
            at = (plane(dz), off(ia, STEPS[n]))
            k = dz * 4 + n
            copy = pltpu.make_async_remote_copy(
                src_ref=tm.at[at], dst_ref=tp.at[at], send_sem=ts_s.at[k], recv_sem=ts_r.at[k],
                device_id=partner, device_id_type=MESH,
            )
            copy.start()
            t_sends.append(copy)

    arrive(0, part(1 - zl, ia, ib, None))
    send_a(1)
    send_b(1, 0)
    relay_a(0)
    relay_b(0, 0)
    relay_a(1)
    relay_b(1, 0)
    far_a(0)
    far_a(1)
    far_b(0, 0)
    far_b(1, 0)
    product([(0, 0), (1, 0)])
    relay_b(0, 1)
    relay_b(0, 2)
    relay_b(1, 1)
    relay_b(1, 2)
    far_b(0, 1)
    far_b(0, 2)
    product([(0, 1), (0, 2)])
    relay_b(0, 3)
    relay_b(1, 3)
    far_b(1, 1)
    far_b(1, 2)
    product([(1, 1), (1, 2)])
    far_b(0, 3)
    far_b(1, 3)
    product([(0, 3), (1, 3)])

    dh, dl = split(z[:, :, :, :, ROWS:WIDE].reshape(DEPTH, HALF))

    for dz in (0, 1):
        for n in range(4):
            k = dz * 4 + n
            ref = tp.at[plane(dz), off(ib, STEPS[n])]
            pltpu.make_async_remote_copy(
                src_ref=ref, dst_ref=ref, send_sem=ts_s.at[k], recv_sem=ts_r.at[k],
                device_id=partner, device_id_type=MESH,
            ).wait_recv()
    for zz in range(2):
        for i in range(4):
            for j in range(4):
                hi, lo = split(tm[zz, i, j] + tp[zz, j, i])
                th[zz, i, j] = hi
                tl[zz, i, j] = lo
    us[...] = dot3(
        dh.T, dl.T, th[...].reshape(DEPTH, COLS), tl[...].reshape(DEPTH, COLS), ((1,), (0,))
    ).reshape(4, 64, COLS)
    u_sends = []
    for i in (1, 0, 2):
        copy = pltpu.make_async_remote_copy(
            src_ref=us.at[(h + i + 1) % 4], dst_ref=ur.at[i], send_sem=us_s.at[i], recv_sem=us_r.at[i],
            device_id=group[i], device_id_type=MESH,
        )
        copy.start()
        u_sends.append(copy)

    for i in range(3):
        ref = ra.at[(h + 3 - i) % 4]
        pltpu.make_async_remote_copy(
            src_ref=ref, dst_ref=ref, send_sem=rs_s.at[i], recv_sem=rs_r.at[i],
            device_id=group[i], device_id_type=MESH,
        ).wait_recv()
    rh, rl = split(ra[...].reshape(HALF, COLS))
    wm[...] = dot3(dh, dl, rh, rl, ((1,), (0,))).reshape(2, 4, 4, 16, COLS)
    w_copy = pltpu.make_async_remote_copy(
        src_ref=wm, dst_ref=wp, send_sem=ws.at[0], recv_sem=ws.at[1], device_id=partner, device_id_type=MESH
    )
    w_copy.start()
    w_copy.wait_recv()
    for zz in range(2):
        for i in range(4):
            for j in range(4):
                hi, lo = split(wm[zz, i, j] + wp[zz, j, i])
                wh[zz, i, j] = hi
                wl[zz, i, j] = lo
    l_adj.wait()
    wth = wh[...].reshape(DEPTH, COLS).T
    wtl = wl[...].reshape(DEPTH, COLS).T
    outs = []
    for j in range(7):
        cut = pl.ds(256 * j, 256)
        pj = ph[:, :, :, :, cut].reshape(DEPTH, 256)
        qj = pL[:, :, :, :, cut].reshape(DEPTH, 256)
        abuf[:, cut] = abuf[:, cut] - dot3(wth, wtl, pj, qj, ((1,), (0,)))
        copy = pltpu.make_async_copy(abuf.at[:, cut], out.at[:, cut], outsem.at[j])
        copy.start()
        outs.append(copy)

    for i in range(3):
        pltpu.make_async_remote_copy(
            src_ref=ur.at[i], dst_ref=ur.at[i], send_sem=us_s.at[i], recv_sem=us_r.at[i],
            device_id=group[i], device_id_type=MESH,
        ).wait_recv()
    radj[...] = us[h] + ur[0] + ur[1] + ur[2]
    for copy in sends + r_sends + t_sends + u_sends + [w_copy]:
        copy.wait_send()
    for copy in outs:
        copy.wait()


def local(panel_adj, inv_diag, row_panel, trailing_adj, trailing_factor):
    dma = pltpu.SemaphoreType.DMA
    any_ = pl.BlockSpec(memory_space=pl.ANY)
    v = pltpu.VMEM
    out, radj = pl.pallas_call(
        kernel,
        out_shape=(
            jax.ShapeDtypeStruct((COLS, ROWS), f32),
            jax.ShapeDtypeStruct((64, COLS), f32),
        ),
        in_specs=[any_] * 5,
        out_specs=(any_, pl.BlockSpec(memory_space=pltpu.VMEM)),
        scratch_shapes=[
            v((2, 4, 4, KS, WIDE), f32),
            v((COLS, ROWS), f32),
            v((COLS, ROWS), bf16),
            v((COLS, ROWS), bf16),
            v((COLS, ROWS), f32),
            v((2, 4, 4, KS, ROWS), bf16),
            v((2, 4, 4, KS, ROWS), bf16),
            v((KS, DEPTH), f32),
            v((4, 64, COLS), f32),
            v((2, 4, 4, KS, COLS), f32),
            v((2, 4, 4, KS, COLS), f32),
            v((2, 4, 4, KS, COLS), bf16),
            v((2, 4, 4, KS, COLS), bf16),
            v((2, 4, 4, KS, COLS), f32),
            v((2, 4, 4, KS, COLS), f32),
            v((2, 4, 4, KS, COLS), bf16),
            v((2, 4, 4, KS, COLS), bf16),
            v((4, 64, COLS), f32),
            v((3, 64, COLS), f32),
            dma((41,)),
            dma((41,)),
            dma((3,)),
            dma((3,)),
            dma((8,)),
            dma((8,)),
            dma((2,)),
            dma((3,)),
            dma((3,)),
            dma((5,)),
            dma((7,)),
        ],
        compiler_params=pltpu.CompilerParams(
            collective_id=0, has_side_effects=True, vmem_limit_bytes=60 * 1024 * 1024
        ),
    )(panel_adj.T, inv_diag, row_panel, trailing_adj.T, trailing_factor.T)
    return out.T, radj


def solution(mesh):
    placed = (P("row", "col"), P("col", None), P("row", "col"), P("row", "col"), P("row", "col"))
    return jax.shard_map(
        local,
        mesh=mesh,
        in_specs=placed,
        out_specs=(P("row", "col"), P("row", "col")),
        check_vma=False,
    )
```

```python
import jax
import jax.numpy as jnp
from jax import lax
from jax.experimental import pallas as pl
from jax.experimental.pallas import tpu as pltpu
from jax.sharding import PartitionSpec as P

MESH = pl.DeviceIdType.MESH
f32, bf16 = jnp.float32, jnp.bfloat16
ROWS, COLS, DEPTH, KS, HALF = 1792, 448, 512, 16, 256
WIDE = ROWS + HALF
STEPS = (0, 3, 1, 2)


def split(v):
    hi = v.astype(bf16)
    return hi, (v - hi.astype(f32)).astype(bf16)


def dot(a, b, dims):
    return lax.dot_general(a, b, (dims, ((), ())), preferred_element_type=f32)


def dot3(ah, al, bh, bl, dims):
    rows = ah.shape[0]
    both = dot(jnp.concatenate([ah, al], axis=0), bh, dims)
    return both[:rows] + both[rows:] + dot(ah, bl, dims)


def kernel(
    panel, inv, rowp, adj, fac, out, radj,
    z, fbuf, fh, fl, abuf, ph, pL, dbuf, ra, tm, tp, th, tl, wm, wp, wh, wl, us, ur,
    ssem, rsem, rs_s, rs_r, ts_s, ts_r, ws, us_s, us_r, loc,
):
    row, col = lax.axis_index("row"), lax.axis_index("col")
    h, core = row // 2, row % 2
    zl, x, y = col // 16, (col // 4) % 4, col % 4
    ia = x + core * (y - x)
    ib = y + core * (x - y)

    def device(zz, a, b):
        return (row, zz * 16 + a * (4 - 3 * core) + b * (1 + 3 * core))

    def off(i, d):
        return (i + d) % 4

    mate = device(1 - zl, ia, ib)
    ap, am = device(zl, off(ia, 1), ib), device(zl, off(ia, 3), ib)
    bp, bm = device(zl, ia, off(ib, 1)), device(zl, ia, off(ib, 3))
    partner = (2 * h + 1 - core, col)
    group = [(2 * ((h + d) % 4) + core, col) for d in (1, 3)]

    def plane(dz):
        return zl if dz == 0 else 1 - zl

    own = z.at[zl, ia, ib]
    l_panel = pltpu.make_async_copy(panel, own.at[:, pl.ds(0, ROWS)], loc.at[0])
    l_inv = pltpu.make_async_copy(inv, dbuf, loc.at[1])
    l_row = pltpu.make_async_copy(rowp, ra.at[h], loc.at[2])
    l_fac = pltpu.make_async_copy(fac, fbuf, loc.at[3])
    l_adj = pltpu.make_async_copy(adj, abuf, loc.at[4])
    l_inv.start()
    l_panel.start()
    l_row.start()
    l_fac.start()
    l_adj.start()

    barrier = pltpu.get_barrier_semaphore()
    others = [mate, ap, am, bp, bm, partner] + group
    for other in others:
        pl.semaphore_signal(barrier, inc=1, device_id=other, device_id_type=MESH)
    l_inv.wait()
    d = dbuf[...]
    even = jnp.concatenate([d[:, 128 * i : 128 * i + 64] for i in range(4)], axis=1)
    odd = jnp.concatenate([d[:, 128 * i + 64 : 128 * i + 128] for i in range(4)], axis=1)
    z[zl, ia, ib, :, ROWS:WIDE] = jnp.where(core == 0, even, odd)
    l_panel.wait()
    l_row.wait()
    pl.semaphore_wait(barrier, len(others))

    sends = []

    def kind_b(dz, n, m):
        return 8 + (dz * 4 + n) * 4 + m

    def part(zz, a, b, half):
        ref = z.at[zz, a, b]
        return ref if half is None else ref.at[pl.ds(8 * half, 8)]

    def send(kind, ref, target):
        copy = pltpu.make_async_remote_copy(
            src_ref=ref, dst_ref=ref, send_sem=ssem.at[kind], recv_sem=rsem.at[kind],
            device_id=target, device_id_type=MESH,
        )
        copy.start()
        sends.append(copy)

    def arrive(kind, ref):
        pltpu.make_async_remote_copy(
            src_ref=ref, dst_ref=ref, send_sem=ssem.at[kind], recv_sem=rsem.at[kind],
            device_id=mate, device_id_type=MESH,
        ).wait_recv()

    def line(dz, n):
        return part(plane(dz), off(ia, STEPS[n]), ib, None)

    def send_b(dz, n):
        send(kind_b(dz, n, 0), line(dz, n), bp)
        send(kind_b(dz, n, 1), line(dz, n), bm)

    def send_z(n):
        send(n, line(0, n), mate)

    def from_z(n):
        arrive(n, line(1, n))
        send_b(1, n)

    def relay_a(m):
        arrive(4 + m, line(0, 1 + m))
        send(6 + m, part(zl, off(ia, STEPS[1 + m]), ib, m), ap if m == 0 else am)
        send_b(0, 1 + m)
        send_z(1 + m)

    def relay_b(dz, n):
        a = off(ia, STEPS[n])
        for m, target in ((0, bp), (1, bm)):
            b = off(ib, STEPS[1 + m])
            arrive(kind_b(dz, n, m), part(plane(dz), a, b, None))
            send(kind_b(dz, n, 2 + m), part(plane(dz), a, b, m), target)

    def far_b(dz, n):
        for m in (0, 1):
            arrive(kind_b(dz, n, 2 + m), part(plane(dz), off(ia, STEPS[n]), off(ib, 2), m))

    hs = [off(h, d) for d in (0, 1, 2, 3)]
    nxt, prv = (2 * hs[1] + core, col), (2 * hs[3] + core, col)
    r_sends = []

    def r_copy(k, ref, target):
        return pltpu.make_async_remote_copy(
            src_ref=ref, dst_ref=ref, send_sem=rs_s.at[k], recv_sem=rs_r.at[k],
            device_id=target, device_id_type=MESH,
        )

    def r_send(k, ref, target):
        copy = r_copy(k, ref, target)
        copy.start()
        r_sends.append(copy)

    def r_own():
        r_send(0, ra.at[h], nxt)
        r_send(1, ra.at[h], prv)

    def r_relay():
        r_copy(0, ra.at[hs[3]], nxt).wait_recv()
        r_send(2, ra.at[hs[3], pl.ds(0, 32)], nxt)
        r_copy(1, ra.at[hs[1]], nxt).wait_recv()
        r_send(3, ra.at[hs[1], pl.ds(32, 32)], prv)

    def r_far():
        r_copy(2, ra.at[hs[2], pl.ds(0, 32)], nxt).wait_recv()
        r_copy(3, ra.at[hs[2], pl.ds(32, 32)], nxt).wait_recv()

    def split_factor():
        l_fac.wait()
        for j in range(7):
            cut = pl.ds(256 * j, 256)
            hi, lo = split(fbuf[:, cut])
            fh[:, cut] = hi
            fl[:, cut] = lo

    t_sends = []

    def product(pieces):
        at = [(plane(dz), off(ib, STEPS[m])) for dz, m in pieces]
        v = jnp.concatenate([z[zz, :, b, :, 0:ROWS].reshape(64, ROWS) for zz, b in at], axis=0)
        hi, lo = split(v)
        for i, (zz, b) in enumerate(at):
            ph[zz, :, b] = hi[64 * i : 64 * i + 64].reshape(4, 16, ROWS)
            pL[zz, :, b] = lo[64 * i : 64 * i + 64].reshape(4, 16, ROWS)
        t = dot3(hi, lo, fh[...], fl[...], ((1,), (1,)))
        for i, (zz, b) in enumerate(at):
            tm[zz, :, b] = t[64 * i : 64 * i + 64].reshape(4, 16, COLS)
        for (dz, m), (zz, b) in zip(pieces, at):
            k = dz * 4 + m
            copy = pltpu.make_async_remote_copy(
                src_ref=tm.at[zz, :, b], dst_ref=tp.at[zz, :, b], send_sem=ts_s.at[k], recv_sem=ts_r.at[k],
                device_id=partner, device_id_type=MESH,
            )
            copy.start()
            t_sends.append(copy)

    send_z(0)
    send(4, line(0, 0), ap)
    send(5, line(0, 0), am)
    send_b(0, 0)
    relay_a(0)
    relay_a(1)
    from_z(0)
    arrive(6, part(zl, off(ia, 2), ib, 0))
    arrive(7, part(zl, off(ia, 2), ib, 1))
    send_b(0, 3)
    send_z(3)
    r_own()
    relay_b(0, 0)
    from_z(1)
    from_z(2)
    relay_b(0, 1)
    relay_b(0, 2)
    from_z(3)
    relay_b(1, 0)
    split_factor()
    relay_b(0, 3)
    product([(0, 0), (1, 0)])
    relay_b(1, 1)
    relay_b(1, 2)
    product([(0, 1), (0, 2)])
    r_relay()
    relay_b(1, 3)
    product([(1, 1), (1, 2)])
    for n in range(4):
        far_b(0, n)
    for n in range(4):
        far_b(1, n)
    product([(0, 3), (1, 3)])

    dh, dl = split(z[:, :, :, :, ROWS:WIDE].reshape(DEPTH, HALF))

    for dz in (0, 1):
        for n in range(4):
            k = dz * 4 + n
            ref = tp.at[plane(dz), :, off(ia, STEPS[n])]
            pltpu.make_async_remote_copy(
                src_ref=ref, dst_ref=ref, send_sem=ts_s.at[k], recv_sem=ts_r.at[k],
                device_id=partner, device_id_type=MESH,
            ).wait_recv()
    for zz in range(2):
        for i in range(4):
            for j in range(4):
                hi, lo = split(tm[zz, i, j] + tp[zz, j, i])
                th[zz, i, j] = hi
                tl[zz, i, j] = lo
    us[...] = dot3(
        dh.T, dl.T, th[...].reshape(DEPTH, COLS), tl[...].reshape(DEPTH, COLS), ((1,), (0,))
    ).reshape(4, 64, COLS)
    u_sends = []

    def u_copy(k, src, target):
        return pltpu.make_async_remote_copy(
            src_ref=src, dst_ref=ur.at[k], send_sem=us_s.at[k], recv_sem=us_r.at[k],
            device_id=target, device_id_type=MESH,
        )

    def u_send(k, block, half, target):
        copy = u_copy(k, us.at[block, pl.ds(32 * half, 32)], target)
        copy.start()
        u_sends.append(copy)

    def u_arrive(k):
        u_copy(k, us.at[h, pl.ds(0, 32)], nxt).wait_recv()

    u_send(0, hs[2], 0, nxt)
    u_send(1, hs[2], 1, prv)
    u_send(2, hs[1], 1, nxt)
    u_send(3, hs[3], 0, prv)

    r_far()
    rh, rl = split(ra[...].reshape(HALF, COLS))
    wm[...] = dot3(dh, dl, rh, rl, ((1,), (0,))).reshape(2, 4, 4, 16, COLS)
    w_copy = pltpu.make_async_remote_copy(
        src_ref=wm, dst_ref=wp, send_sem=ws.at[0], recv_sem=ws.at[1], device_id=partner, device_id_type=MESH
    )
    w_copy.start()
    w_copy.wait_recv()
    for zz in range(2):
        for i in range(4):
            for j in range(4):
                hi, lo = split(wm[zz, i, j] + wp[zz, j, i])
                wh[zz, i, j] = hi
                wl[zz, i, j] = lo
    u_arrive(0)
    us[hs[1], 0:32] += ur[0]
    u_send(4, hs[1], 0, nxt)
    u_arrive(1)
    us[hs[3], 32:64] += ur[1]
    u_send(5, hs[3], 1, prv)
    l_adj.wait()
    wth = wh[...].reshape(DEPTH, COLS).T
    wtl = wl[...].reshape(DEPTH, COLS).T
    for j in range(7):
        cut = pl.ds(256 * j, 256)
        pj = ph[:, :, :, :, cut].reshape(DEPTH, 256)
        qj = pL[:, :, :, :, cut].reshape(DEPTH, 256)
        out[:, cut] = abuf[:, cut] - dot3(wth, wtl, pj, qj, ((1,), (0,)))

    for k in (2, 3, 4, 5):
        u_arrive(k)
    radj[0:32] = us[h, 0:32] + ur[4] + ur[3]
    radj[32:64] = us[h, 32:64] + ur[2] + ur[5]
    for copy in sends + r_sends + t_sends + u_sends + [w_copy]:
        copy.wait_send()


def local(panel_adj, inv_diag, row_panel, trailing_adj, trailing_factor):
    dma = pltpu.SemaphoreType.DMA
    hbm = pl.BlockSpec(memory_space=pltpu.HBM)
    v = pltpu.VMEM
    out, radj = pl.pallas_call(
        kernel,
        out_shape=(
            v((COLS, ROWS), f32),
            v((64, COLS), f32),
        ),
        in_specs=[hbm] * 5,
        out_specs=(pl.BlockSpec(memory_space=pltpu.VMEM),) * 2,
        scratch_shapes=[
            v((2, 4, 4, KS, WIDE), f32),
            v((COLS, ROWS), f32),
            v((COLS, ROWS), bf16),
            v((COLS, ROWS), bf16),
            v((COLS, ROWS), f32),
            v((2, 4, 4, KS, ROWS), bf16),
            v((2, 4, 4, KS, ROWS), bf16),
            v((KS, DEPTH), f32),
            v((4, 64, COLS), f32),
            v((2, 4, 4, KS, COLS), f32),
            v((2, 4, 4, KS, COLS), f32),
            v((2, 4, 4, KS, COLS), bf16),
            v((2, 4, 4, KS, COLS), bf16),
            v((2, 4, 4, KS, COLS), f32),
            v((2, 4, 4, KS, COLS), f32),
            v((2, 4, 4, KS, COLS), bf16),
            v((2, 4, 4, KS, COLS), bf16),
            v((4, 64, COLS), f32),
            v((6, 32, COLS), f32),
            dma((40,)),
            dma((40,)),
            dma((4,)),
            dma((4,)),
            dma((8,)),
            dma((8,)),
            dma((2,)),
            dma((6,)),
            dma((6,)),
            dma((5,)),
        ],
        compiler_params=pltpu.CompilerParams(
            collective_id=0, has_side_effects=True, vmem_limit_bytes=63_500_000
        ),
    )(panel_adj.T, inv_diag, row_panel, trailing_adj.T, trailing_factor.T)
    return out.T, radj


def solution(mesh):
    placed = (P("row", "col"), P("col", None), P("row", "col"), P("row", "col"), P("row", "col"))
    return jax.shard_map(
        local,
        mesh=mesh,
        in_specs=placed,
        out_specs=(P("row", "col"), P("row", "col")),
        check_vma=False,
    )
```

```python
import jax
import jax.numpy as jnp
from jax import lax
from jax.experimental import pallas as pl
from jax.experimental.pallas import tpu as pltpu
from jax.sharding import PartitionSpec as P

MESH = pl.DeviceIdType.MESH
f32, bf16 = jnp.float32, jnp.bfloat16
ROWS, COLS, DEPTH, KS, HALF = 1792, 448, 512, 16, 256
WIDE = ROWS + HALF
STEPS = (0, 3, 1, 2)


def split(v):
    hi = v.astype(bf16)
    return hi, (v - hi.astype(f32)).astype(bf16)


def dot(a, b, dims):
    return lax.dot_general(a, b, (dims, ((), ())), preferred_element_type=f32)


def dot3(ah, al, bh, bl, dims):
    rows = ah.shape[0]
    both = dot(jnp.concatenate([ah, al], axis=0), bh, dims)
    return both[:rows] + both[rows:] + dot(ah, bl, dims)


def kernel(
    panel, inv, rowp, adj, fac, out, radj,
    z, fbuf, fh, fl, abuf, ph, pL, dbuf, ra, tm, tp, th, tl, wm, wp, wh, wl, us, ur,
    ssem, rsem, rs_s, rs_r, ts_s, ts_r, ws, us_s, us_r, loc,
):
    row, col = lax.axis_index("row"), lax.axis_index("col")
    h, core = row // 2, row % 2
    zl, x, y = col // 16, (col // 4) % 4, col % 4
    ia = x + core * (y - x)
    ib = y + core * (x - y)

    def device(zz, a, b):
        return (row, zz * 16 + a * (4 - 3 * core) + b * (1 + 3 * core))

    def off(i, d):
        return (i + d) % 4

    mate = device(1 - zl, ia, ib)
    ap, am = device(zl, off(ia, 1), ib), device(zl, off(ia, 3), ib)
    bp, bm = device(zl, ia, off(ib, 1)), device(zl, ia, off(ib, 3))
    partner = (2 * h + 1 - core, col)
    group = [(2 * ((h + d) % 4) + core, col) for d in (1, 3)]

    def plane(dz):
        return zl if dz == 0 else 1 - zl

    own = z.at[zl, ia, ib]
    l_panel = pltpu.make_async_copy(panel, own.at[:, pl.ds(0, ROWS)], loc.at[0])
    l_inv = pltpu.make_async_copy(inv, dbuf, loc.at[1])
    l_row = pltpu.make_async_copy(rowp, ra.at[h], loc.at[2])
    l_fac = pltpu.make_async_copy(fac, fbuf, loc.at[3])
    l_adj = pltpu.make_async_copy(adj, abuf, loc.at[4])
    barrier = pltpu.get_barrier_semaphore()
    others = [mate, ap, am, bp, bm, partner] + group
    for other in others:
        pl.semaphore_signal(barrier, inc=1, device_id=other, device_id_type=MESH)
    l_inv.start()
    l_panel.start()
    l_row.start()
    l_inv.wait()
    d = dbuf[...]
    even = jnp.concatenate([d[:, 128 * i : 128 * i + 64] for i in range(4)], axis=1)
    odd = jnp.concatenate([d[:, 128 * i + 64 : 128 * i + 128] for i in range(4)], axis=1)
    z[zl, ia, ib, :, ROWS:WIDE] = jnp.where(core == 0, even, odd)
    l_panel.wait()
    pl.semaphore_wait(barrier, len(others))

    sends = []

    def kind_b(dz, n, m):
        return 11 + (dz * 4 + n) * 4 + m

    def part(zz, a, b, half):
        ref = z.at[zz, a, b]
        return ref if half is None else ref.at[pl.ds(8 * half, 8)]

    def send(kind, ref, target):
        copy = pltpu.make_async_remote_copy(
            src_ref=ref, dst_ref=ref, send_sem=ssem.at[kind], recv_sem=rsem.at[kind],
            device_id=target, device_id_type=MESH,
        )
        copy.start()
        sends.append(copy)
        return copy

    def arrive(kind, ref):
        pltpu.make_async_remote_copy(
            src_ref=ref, dst_ref=ref, send_sem=ssem.at[kind], recv_sem=rsem.at[kind],
            device_id=mate, device_id_type=MESH,
        ).wait_recv()

    def line(dz, n):
        return part(plane(dz), off(ia, STEPS[n]), ib, None)

    def send_b(dz, n):
        send(kind_b(dz, n, 0), line(dz, n), bp)
        send(kind_b(dz, n, 1), line(dz, n), bm)

    def half(dz, m):
        return part(plane(dz), off(ia, STEPS[1 + m]), ib, m)

    def other_half(dz, m):
        return part(plane(dz), off(ia, STEPS[1 + m]), ib, 1 - m)

    def onward(m):
        return ap if m == 0 else am

    def relay_a(m):
        arrive(3 + m, line(0, 1 + m))
        send(5 + m, half(0, m), onward(m))
        send(1 + m, other_half(0, m), mate)
        send_b(0, 1 + m)

    def from_mate():
        arrive(0, line(1, 0))
        for m in (0, 1):
            send(7 + m, part(1 - zl, ia, ib, m), onward(m))
        send_b(1, 0)

    def relay_mate(m):
        arrive(7 + m, half(1, m))
        send(9 + m, half(1, m), onward(m))

    def from_z(m):
        arrive(1 + m, other_half(1, m))
        send_b(1, 1 + m)

    def far_a(dz):
        for m in (0, 1):
            arrive((5 if dz == 0 else 9) + m, part(plane(dz), off(ia, 2), ib, m))
        send_b(dz, 3)

    def relay_b(dz, n):
        a = off(ia, STEPS[n])
        for m, target in ((0, bp), (1, bm)):
            b = off(ib, STEPS[1 + m])
            arrive(kind_b(dz, n, m), part(plane(dz), a, b, None))
            send(kind_b(dz, n, 2 + m), part(plane(dz), a, b, m), target)

    def far_b(dz, n):
        for m in (0, 1):
            arrive(kind_b(dz, n, 2 + m), part(plane(dz), off(ia, STEPS[n]), off(ib, 2), m))

    hs = [off(h, d) for d in (0, 1, 2, 3)]
    nxt, prv = (2 * hs[1] + core, col), (2 * hs[3] + core, col)
    r_sends = []

    def r_copy(k, ref, target):
        return pltpu.make_async_remote_copy(
            src_ref=ref, dst_ref=ref, send_sem=rs_s.at[k], recv_sem=rs_r.at[k],
            device_id=target, device_id_type=MESH,
        )

    def r_send(k, ref, target):
        copy = r_copy(k, ref, target)
        copy.start()
        r_sends.append(copy)

    def r_own():
        l_row.wait()
        r_send(0, ra.at[h], nxt)
        r_send(1, ra.at[h], prv)

    def r_relay():
        r_copy(0, ra.at[hs[3]], nxt).wait_recv()
        r_send(2, ra.at[hs[3], pl.ds(0, 32)], nxt)
        r_copy(1, ra.at[hs[1]], nxt).wait_recv()
        r_send(3, ra.at[hs[1], pl.ds(32, 32)], prv)

    def r_far():
        r_copy(2, ra.at[hs[2], pl.ds(0, 32)], nxt).wait_recv()
        r_copy(3, ra.at[hs[2], pl.ds(32, 32)], nxt).wait_recv()

    def split_factor():
        l_fac.wait()
        for j in range(7):
            cut = pl.ds(256 * j, 256)
            hi, lo = split(fbuf[:, cut])
            fh[:, cut] = hi
            fl[:, cut] = lo

    t_sends = []

    def product(pieces):
        at = [(plane(dz), off(ib, STEPS[m])) for dz, m in pieces]
        v = jnp.concatenate([z[zz, :, b, :, 0:ROWS].reshape(64, ROWS) for zz, b in at], axis=0)
        hi, lo = split(v)
        for i, (zz, b) in enumerate(at):
            ph[zz, :, b] = hi[64 * i : 64 * i + 64].reshape(4, 16, ROWS)
            pL[zz, :, b] = lo[64 * i : 64 * i + 64].reshape(4, 16, ROWS)
        t = dot3(hi, lo, fh[...], fl[...], ((1,), (1,)))
        for i, (zz, b) in enumerate(at):
            tm[zz, :, b] = t[64 * i : 64 * i + 64].reshape(4, 16, COLS)
        for (dz, m), (zz, b) in zip(pieces, at):
            k = dz * 4 + m
            copy = pltpu.make_async_remote_copy(
                src_ref=tm.at[zz, :, b], dst_ref=tp.at[zz, :, b], send_sem=ts_s.at[k], recv_sem=ts_r.at[k],
                device_id=partner, device_id_type=MESH,
            )
            copy.start()
            t_sends.append(copy)

    def t_wait(dz, m):
        ref = tp.at[plane(dz), :, off(ia, STEPS[m])]
        k = dz * 4 + m
        pltpu.make_async_remote_copy(
            src_ref=ref, dst_ref=ref, send_sem=ts_s.at[k], recv_sem=ts_r.at[k],
            device_id=partner, device_id_type=MESH,
        ).wait_recv()

    def t_sum(n, m):
        a, b = off(ia, STEPS[n]), off(ib, STEPS[m])
        for zz in range(2):
            hi, lo = split(tm[zz, a, b] + tp[zz, b, a])
            th[zz, a, b] = hi
            tl[zz, a, b] = lo

    first = send(3, line(0, 0), ap)
    send(4, line(0, 0), am)
    send(0, line(0, 0), mate)
    l_fac.start()
    l_adj.start()
    first.wait_send()
    del sends[0]
    send_b(0, 0)
    relay_a(0)
    relay_a(1)
    from_mate()
    r_own()
    relay_b(0, 0)
    split_factor()
    relay_mate(0)
    relay_mate(1)
    far_a(0)
    from_z(0)
    from_z(1)
    relay_b(0, 1)
    relay_b(0, 2)
    far_a(1)
    relay_b(1, 0)
    relay_b(0, 3)
    product([(0, 0), (0, 1)])
    relay_b(1, 1)
    relay_b(1, 2)
    product([(0, 2), (1, 0)])
    r_relay()
    relay_b(1, 3)
    product([(1, 1), (1, 2)])
    for n in range(4):
        far_b(0, n)
    product([(0, 3)])
    for dz in (0, 1):
        for m in (0, 1, 2):
            t_wait(dz, m)
    for n in (0, 1, 2):
        for m in (0, 1, 2):
            t_sum(n, m)
    for n in range(4):
        far_b(1, n)
    product([(1, 3)])

    dh, dl = split(z[:, :, :, :, ROWS:WIDE].reshape(DEPTH, HALF))

    t_wait(0, 3)
    t_wait(1, 3)
    for n in range(4):
        for m in range(4):
            if n == 3 or m == 3:
                t_sum(n, m)
    us[...] = dot3(
        dh.T, dl.T, th[...].reshape(DEPTH, COLS), tl[...].reshape(DEPTH, COLS), ((1,), (0,))
    ).reshape(4, 64, COLS)
    u_sends = []

    def u_copy(k, src, target):
        return pltpu.make_async_remote_copy(
            src_ref=src, dst_ref=ur.at[k], send_sem=us_s.at[k], recv_sem=us_r.at[k],
            device_id=target, device_id_type=MESH,
        )

    def u_send(k, block, half, target):
        copy = u_copy(k, us.at[block, pl.ds(32 * half, 32)], target)
        copy.start()
        u_sends.append(copy)

    def u_arrive(k):
        u_copy(k, us.at[h, pl.ds(0, 32)], nxt).wait_recv()

    u_send(0, hs[2], 0, nxt)
    u_send(1, hs[2], 1, prv)
    u_send(2, hs[1], 1, nxt)
    u_send(3, hs[3], 0, prv)

    r_far()
    rh, rl = split(ra[...].reshape(HALF, COLS))
    wm[...] = dot3(dh, dl, rh, rl, ((1,), (0,))).reshape(2, 4, 4, 16, COLS)
    w_copy = pltpu.make_async_remote_copy(
        src_ref=wm, dst_ref=wp, send_sem=ws.at[0], recv_sem=ws.at[1], device_id=partner, device_id_type=MESH
    )
    w_copy.start()
    u_arrive(0)
    us[hs[1], 0:32] += ur[0]
    u_send(4, hs[1], 0, nxt)
    u_arrive(1)
    us[hs[3], 32:64] += ur[1]
    u_send(5, hs[3], 1, prv)
    w_copy.wait_recv()
    for zz in range(2):
        for i in range(4):
            for j in range(4):
                hi, lo = split(wm[zz, i, j] + wp[zz, j, i])
                wh[zz, i, j] = hi
                wl[zz, i, j] = lo
    l_adj.wait()
    wth = wh[...].reshape(DEPTH, COLS).T
    wtl = wl[...].reshape(DEPTH, COLS).T
    for j in range(7):
        cut = pl.ds(256 * j, 256)
        pj = ph[:, :, :, :, cut].reshape(DEPTH, 256)
        qj = pL[:, :, :, :, cut].reshape(DEPTH, 256)
        out[:, cut] = abuf[:, cut] - dot3(wth, wtl, pj, qj, ((1,), (0,)))

    for k in (2, 3, 4, 5):
        u_arrive(k)
    radj[0:32] = us[h, 0:32] + ur[4] + ur[3]
    radj[32:64] = us[h, 32:64] + ur[2] + ur[5]
    for copy in sends + r_sends + t_sends + u_sends + [w_copy]:
        copy.wait_send()


def finish(a, b, out_a, out_b, sem):
    copies = [pltpu.make_async_copy(b, out_b, sem.at[7])]
    for j in range(7):
        cut = pl.ds(64 * j, 64)
        copies.append(pltpu.make_async_copy(a.at[cut], out_a.at[cut], sem.at[j]))
    for copy in copies:
        copy.start()
    for copy in copies:
        copy.wait()


def local(panel_adj, inv_diag, row_panel, trailing_adj, trailing_factor):
    dma = pltpu.SemaphoreType.DMA
    hbm = pl.BlockSpec(memory_space=pltpu.HBM)
    v = pltpu.VMEM
    out, radj = pl.pallas_call(
        kernel,
        out_shape=(
            v((COLS, ROWS), f32),
            v((64, COLS), f32),
        ),
        in_specs=[hbm] * 5,
        out_specs=(pl.BlockSpec(memory_space=pltpu.VMEM),) * 2,
        scratch_shapes=[
            v((2, 4, 4, KS, WIDE), f32),
            v((COLS, ROWS), f32),
            v((COLS, ROWS), bf16),
            v((COLS, ROWS), bf16),
            v((COLS, ROWS), f32),
            v((2, 4, 4, KS, ROWS), bf16),
            v((2, 4, 4, KS, ROWS), bf16),
            v((KS, DEPTH), f32),
            v((4, 64, COLS), f32),
            v((2, 4, 4, KS, COLS), f32),
            v((2, 4, 4, KS, COLS), f32),
            v((2, 4, 4, KS, COLS), bf16),
            v((2, 4, 4, KS, COLS), bf16),
            v((2, 4, 4, KS, COLS), f32),
            v((2, 4, 4, KS, COLS), f32),
            v((2, 4, 4, KS, COLS), bf16),
            v((2, 4, 4, KS, COLS), bf16),
            v((4, 64, COLS), f32),
            v((6, 32, COLS), f32),
            dma((43,)),
            dma((43,)),
            dma((4,)),
            dma((4,)),
            dma((8,)),
            dma((8,)),
            dma((2,)),
            dma((6,)),
            dma((6,)),
            dma((5,)),
        ],
        compiler_params=pltpu.CompilerParams(
            collective_id=0, has_side_effects=True, vmem_limit_bytes=63_500_000
        ),
    )(panel_adj.T, inv_diag, row_panel, trailing_adj.T, trailing_factor.T)
    out, radj = pl.pallas_call(
        finish,
        out_shape=(
            jax.ShapeDtypeStruct((COLS, ROWS), f32),
            jax.ShapeDtypeStruct((64, COLS), f32),
        ),
        in_specs=[pl.BlockSpec(memory_space=pl.ANY)] * 2,
        out_specs=(hbm,) * 2,
        scratch_shapes=[dma((8,))],
        compiler_params=pltpu.CompilerParams(vmem_limit_bytes=1024 * 1024),
    )(out, radj)
    return out.T, radj


def solution(mesh):
    placed = (P("row", "col"), P("col", None), P("row", "col"), P("row", "col"), P("row", "col"))
    return jax.shard_map(
        local,
        mesh=mesh,
        in_specs=placed,
        out_specs=(P("row", "col"), P("row", "col")),
        check_vma=False,
    )
```

```python
import jax
import jax.numpy as jnp
from jax import lax
from jax.experimental import pallas as pl
from jax.experimental.pallas import tpu as pltpu
from jax.sharding import PartitionSpec as P

MESH = pl.DeviceIdType.MESH
f32, bf16 = jnp.float32, jnp.bfloat16
ROWS, COLS, DEPTH, KS, HALF = 1792, 448, 512, 16, 256
WIDE = ROWS + HALF
STEPS = (0, 3, 1, 2)


def split(v):
    hi = v.astype(bf16)
    return hi, (v - hi.astype(f32)).astype(bf16)


def dot(a, b, dims):
    return lax.dot_general(a, b, (dims, ((), ())), preferred_element_type=f32)


def dot3(ah, al, bh, bl, dims):
    rows = ah.shape[0]
    both = dot(jnp.concatenate([ah, al], axis=0), bh, dims)
    return both[:rows] + both[rows:] + dot(ah, bl, dims)


def kernel(
    panel, inv, rowp, adj, fac, out, radj,
    z, fbuf, fh, fl, abuf, ph, pL, dbuf, ra, tm, tp, th, tl, wm, wp, wh, wl, us, ur,
    ssem, rsem, rs_s, rs_r, ts_s, ts_r, ws, us_s, us_r, loc,
):
    row, col = lax.axis_index("row"), lax.axis_index("col")
    h, core = row // 2, row % 2
    zl, x, y = col // 16, (col // 4) % 4, col % 4
    ia = x + core * (y - x)
    ib = y + core * (x - y)

    def device(zz, a, b):
        return (row, zz * 16 + a * (4 - 3 * core) + b * (1 + 3 * core))

    def off(i, d):
        return (i + d) % 4

    mate = device(1 - zl, ia, ib)
    ap, am = device(zl, off(ia, 1), ib), device(zl, off(ia, 3), ib)
    bp, bm = device(zl, ia, off(ib, 1)), device(zl, ia, off(ib, 3))
    partner = (2 * h + 1 - core, col)
    group = [(2 * ((h + d) % 4) + core, col) for d in (1, 3)]

    def plane(dz):
        return zl if dz == 0 else 1 - zl

    own = z.at[zl, ia, ib]
    l_panel = pltpu.make_async_copy(panel, own.at[:, pl.ds(0, ROWS)], loc.at[0])
    l_inv = pltpu.make_async_copy(inv, dbuf, loc.at[1])
    l_row = pltpu.make_async_copy(rowp, ra.at[h], loc.at[2])
    l_fac = pltpu.make_async_copy(fac, fbuf, loc.at[3])
    l_adj = pltpu.make_async_copy(adj, abuf, loc.at[4])
    barrier = pltpu.get_barrier_semaphore()
    others = [mate, ap, am, bp, bm, partner] + group
    for other in others:
        pl.semaphore_signal(barrier, inc=1, device_id=other, device_id_type=MESH)
    l_inv.start()
    l_panel.start()
    l_row.start()
    l_inv.wait()
    d = dbuf[...]
    even = jnp.concatenate([d[:, 128 * i : 128 * i + 64] for i in range(4)], axis=1)
    odd = jnp.concatenate([d[:, 128 * i + 64 : 128 * i + 128] for i in range(4)], axis=1)
    z[zl, ia, ib, :, ROWS:WIDE] = jnp.where(core == 0, even, odd)
    l_panel.wait()
    pl.semaphore_wait(barrier, len(others))

    sends = []

    def kind_b(dz, n, m):
        return 11 + (dz * 4 + n) * 4 + m

    def part(zz, a, b, half):
        ref = z.at[zz, a, b]
        return ref if half is None else ref.at[pl.ds(8 * half if isinstance(half, int) else pl.multiple_of(8 * half, 8), 8)]

    wa, wb = 1 - jnp.minimum(ia, 1), 1 - jnp.minimum(ib, 1)

    def side(plus, minus, m):
        return tuple(p + m * (q - p) for p, q in zip(plus, minus))

    def send(kind, ref, target):
        copy = pltpu.make_async_remote_copy(
            src_ref=ref, dst_ref=ref, send_sem=ssem.at[kind], recv_sem=rsem.at[kind],
            device_id=target, device_id_type=MESH,
        )
        copy.start()
        sends.append(copy)
        return copy

    def arrive(kind, ref):
        pltpu.make_async_remote_copy(
            src_ref=ref, dst_ref=ref, send_sem=ssem.at[kind], recv_sem=rsem.at[kind],
            device_id=mate, device_id_type=MESH,
        ).wait_recv()

    def line(dz, n):
        return part(plane(dz), off(ia, STEPS[n]), ib, None)

    def send_b(dz, n):
        send(kind_b(dz, n, 0), line(dz, n), bp)
        send(kind_b(dz, n, 1), line(dz, n), bm)

    def beside(dz, m):
        return part(plane(dz), off(ia, 3 - 2 * m), ib, None)

    def half(dz, m):
        return part(plane(dz), off(ia, 3 - 2 * m), ib, m)

    def other_half(dz, m):
        return part(plane(dz), off(ia, 3 - 2 * m), ib, 1 - m)

    def onward(m):
        return side(ap, am, m)

    def send_beside(dz, m):
        send(kind_b(dz, 1 + m, 0), beside(dz, m), bp)
        send(kind_b(dz, 1 + m, 1), beside(dz, m), bm)

    def relay_a(m):
        arrive(3 + m, beside(0, m))
        send(5 + m, half(0, m), onward(m))
        send(1 + m, other_half(0, m), mate)
        send_beside(0, m)

    def from_mate():
        arrive(0, line(1, 0))
        for m in (0, 1):
            send(7 + m, part(1 - zl, ia, ib, m), onward(m))
        send_b(1, 0)

    def relay_mate(m):
        arrive(7 + m, half(1, m))
        send(9 + m, half(1, m), onward(m))

    def from_z(m):
        arrive(1 + m, other_half(1, m))
        send_beside(1, m)

    def far_a(dz):
        for m in (0, 1):
            arrive((5 if dz == 0 else 9) + m, part(plane(dz), off(ia, 2), ib, m))
        send_b(dz, 3)

    def relay_b(dz, n):
        a = off(ia, STEPS[n])
        for m in (wb, 1 - wb):
            b = off(ib, 3 - 2 * m)
            arrive(kind_b(dz, n, m), part(plane(dz), a, b, None))
            send(kind_b(dz, n, 2 + m), part(plane(dz), a, b, m), side(bp, bm, m))

    def far_b(dz, n):
        for m in (0, 1):
            arrive(kind_b(dz, n, 2 + m), part(plane(dz), off(ia, STEPS[n]), off(ib, 2), m))

    hs = [off(h, d) for d in (0, 1, 2, 3)]
    nxt, prv = (2 * hs[1] + core, col), (2 * hs[3] + core, col)
    r_sends = []

    def r_copy(k, ref, target):
        return pltpu.make_async_remote_copy(
            src_ref=ref, dst_ref=ref, send_sem=rs_s.at[k], recv_sem=rs_r.at[k],
            device_id=target, device_id_type=MESH,
        )

    def r_send(k, ref, target):
        copy = r_copy(k, ref, target)
        copy.start()
        r_sends.append(copy)

    def r_own():
        l_row.wait()
        r_send(0, ra.at[h], nxt)
        r_send(1, ra.at[h], prv)

    def r_relay():
        r_copy(0, ra.at[hs[3]], nxt).wait_recv()
        r_send(2, ra.at[hs[3], pl.ds(0, 32)], nxt)
        r_copy(1, ra.at[hs[1]], nxt).wait_recv()
        r_send(3, ra.at[hs[1], pl.ds(32, 32)], prv)

    def r_far():
        r_copy(2, ra.at[hs[2], pl.ds(0, 32)], nxt).wait_recv()
        r_copy(3, ra.at[hs[2], pl.ds(32, 32)], nxt).wait_recv()

    def split_factor():
        l_fac.wait()
        for j in range(7):
            cut = pl.ds(256 * j, 256)
            hi, lo = split(fbuf[:, cut])
            fh[:, cut] = hi
            fl[:, cut] = lo

    t_sends = []

    def product(pieces):
        at = [(plane(dz), off(ib, STEPS[m])) for dz, m in pieces]
        v = jnp.concatenate([z[zz, :, b, :, 0:ROWS].reshape(64, ROWS) for zz, b in at], axis=0)
        hi, lo = split(v)
        for i, (zz, b) in enumerate(at):
            ph[zz, :, b] = hi[64 * i : 64 * i + 64].reshape(4, 16, ROWS)
            pL[zz, :, b] = lo[64 * i : 64 * i + 64].reshape(4, 16, ROWS)
        t = dot3(hi, lo, fh[...], fl[...], ((1,), (1,)))
        for i, (zz, b) in enumerate(at):
            tm[zz, :, b] = t[64 * i : 64 * i + 64].reshape(4, 16, COLS)
        for (dz, m), (zz, b) in zip(pieces, at):
            k = dz * 4 + m
            copy = pltpu.make_async_remote_copy(
                src_ref=tm.at[zz, :, b], dst_ref=tp.at[zz, :, b], send_sem=ts_s.at[k], recv_sem=ts_r.at[k],
                device_id=partner, device_id_type=MESH,
            )
            copy.start()
            t_sends.append(copy)

    def t_wait(dz, m):
        ref = tp.at[plane(dz), :, off(ia, STEPS[m])]
        k = dz * 4 + m
        pltpu.make_async_remote_copy(
            src_ref=ref, dst_ref=ref, send_sem=ts_s.at[k], recv_sem=ts_r.at[k],
            device_id=partner, device_id_type=MESH,
        ).wait_recv()

    def t_sum(n, m):
        a, b = off(ia, STEPS[n]), off(ib, STEPS[m])
        for zz in range(2):
            hi, lo = split(tm[zz, a, b] + tp[zz, b, a])
            th[zz, a, b] = hi
            tl[zz, a, b] = lo

    first = send(3, line(0, 0), ap)
    send(4, line(0, 0), am)
    send(0, line(0, 0), mate)
    l_fac.start()
    l_adj.start()
    first.wait_send()
    del sends[0]
    send_b(0, 0)
    relay_a(wa)
    relay_a(1 - wa)
    from_mate()
    r_own()
    relay_b(0, 0)
    split_factor()
    relay_mate(wa)
    relay_mate(1 - wa)
    far_a(0)
    from_z(0)
    from_z(1)
    relay_b(0, 1)
    relay_b(0, 2)
    far_a(1)
    relay_b(1, 0)
    relay_b(0, 3)
    product([(0, 0), (0, 1)])
    relay_b(1, 1)
    relay_b(1, 2)
    product([(0, 2), (1, 0)])
    r_relay()
    relay_b(1, 3)
    product([(1, 1), (1, 2)])
    for n in range(4):
        far_b(0, n)
    product([(0, 3)])
    for dz in (0, 1):
        for m in (0, 1, 2):
            t_wait(dz, m)
    for n in (0, 1, 2):
        for m in (0, 1, 2):
            t_sum(n, m)
    for n in range(4):
        far_b(1, n)
    product([(1, 3)])

    dh, dl = split(z[:, :, :, :, ROWS:WIDE].reshape(DEPTH, HALF))

    t_wait(0, 3)
    t_wait(1, 3)
    for n in range(4):
        for m in range(4):
            if n == 3 or m == 3:
                t_sum(n, m)
    us[...] = dot3(
        dh.T, dl.T, th[...].reshape(DEPTH, COLS), tl[...].reshape(DEPTH, COLS), ((1,), (0,))
    ).reshape(4, 64, COLS)
    u_sends = []

    def u_copy(k, src, target):
        return pltpu.make_async_remote_copy(
            src_ref=src, dst_ref=ur.at[k], send_sem=us_s.at[k], recv_sem=us_r.at[k],
            device_id=target, device_id_type=MESH,
        )

    def u_send(k, block, half, target):
        copy = u_copy(k, us.at[block, pl.ds(32 * half, 32)], target)
        copy.start()
        u_sends.append(copy)

    def u_arrive(k):
        u_copy(k, us.at[h, pl.ds(0, 32)], nxt).wait_recv()

    u_send(0, hs[2], 0, nxt)
    u_send(1, hs[2], 1, prv)
    u_send(2, hs[1], 1, nxt)
    u_send(3, hs[3], 0, prv)

    r_far()
    rh, rl = split(ra[...].reshape(HALF, COLS))
    wm[...] = dot3(dh, dl, rh, rl, ((1,), (0,))).reshape(2, 4, 4, 16, COLS)
    w_copy = pltpu.make_async_remote_copy(
        src_ref=wm, dst_ref=wp, send_sem=ws.at[0], recv_sem=ws.at[1], device_id=partner, device_id_type=MESH
    )
    w_copy.start()
    u_arrive(0)
    us[hs[1], 0:32] += ur[0]
    u_send(4, hs[1], 0, nxt)
    u_arrive(1)
    us[hs[3], 32:64] += ur[1]
    u_send(5, hs[3], 1, prv)
    w_copy.wait_recv()
    for zz in range(2):
        for i in range(4):
            for j in range(4):
                hi, lo = split(wm[zz, i, j] + wp[zz, j, i])
                wh[zz, i, j] = hi
                wl[zz, i, j] = lo
    l_adj.wait()
    wth = wh[...].reshape(DEPTH, COLS).T
    wtl = wl[...].reshape(DEPTH, COLS).T
    for j in range(7):
        cut = pl.ds(256 * j, 256)
        pj = ph[:, :, :, :, cut].reshape(DEPTH, 256)
        qj = pL[:, :, :, :, cut].reshape(DEPTH, 256)
        out[:, cut] = abuf[:, cut] - dot3(wth, wtl, pj, qj, ((1,), (0,)))

    for k in (2, 3, 4, 5):
        u_arrive(k)
    radj[0:32] = us[h, 0:32] + ur[4] + ur[3]
    radj[32:64] = us[h, 32:64] + ur[2] + ur[5]
    for copy in sends + r_sends + t_sends + u_sends + [w_copy]:
        copy.wait_send()


def finish(a, b, out_a, out_b, sem):
    copies = [pltpu.make_async_copy(b, out_b, sem.at[7])]
    for j in range(7):
        cut = pl.ds(64 * j, 64)
        copies.append(pltpu.make_async_copy(a.at[cut], out_a.at[cut], sem.at[j]))
    for copy in copies:
        copy.start()
    for copy in copies:
        copy.wait()


def local(panel_adj, inv_diag, row_panel, trailing_adj, trailing_factor):
    dma = pltpu.SemaphoreType.DMA
    hbm = pl.BlockSpec(memory_space=pltpu.HBM)
    v = pltpu.VMEM
    out, radj = pl.pallas_call(
        kernel,
        out_shape=(
            v((COLS, ROWS), f32),
            v((64, COLS), f32),
        ),
        in_specs=[hbm] * 5,
        out_specs=(pl.BlockSpec(memory_space=pltpu.VMEM),) * 2,
        scratch_shapes=[
            v((2, 4, 4, KS, WIDE), f32),
            v((COLS, ROWS), f32),
            v((COLS, ROWS), bf16),
            v((COLS, ROWS), bf16),
            v((COLS, ROWS), f32),
            v((2, 4, 4, KS, ROWS), bf16),
            v((2, 4, 4, KS, ROWS), bf16),
            v((KS, DEPTH), f32),
            v((4, 64, COLS), f32),
            v((2, 4, 4, KS, COLS), f32),
            v((2, 4, 4, KS, COLS), f32),
            v((2, 4, 4, KS, COLS), bf16),
            v((2, 4, 4, KS, COLS), bf16),
            v((2, 4, 4, KS, COLS), f32),
            v((2, 4, 4, KS, COLS), f32),
            v((2, 4, 4, KS, COLS), bf16),
            v((2, 4, 4, KS, COLS), bf16),
            v((4, 64, COLS), f32),
            v((6, 32, COLS), f32),
            dma((43,)),
            dma((43,)),
            dma((4,)),
            dma((4,)),
            dma((8,)),
            dma((8,)),
            dma((2,)),
            dma((6,)),
            dma((6,)),
            dma((5,)),
        ],
        compiler_params=pltpu.CompilerParams(
            collective_id=0, has_side_effects=True, vmem_limit_bytes=63_500_000
        ),
    )(panel_adj.T, inv_diag, row_panel, trailing_adj.T, trailing_factor.T)
    out, radj = pl.pallas_call(
        finish,
        out_shape=(
            jax.ShapeDtypeStruct((COLS, ROWS), f32),
            jax.ShapeDtypeStruct((64, COLS), f32),
        ),
        in_specs=[pl.BlockSpec(memory_space=pl.ANY)] * 2,
        out_specs=(hbm,) * 2,
        scratch_shapes=[dma((8,))],
        compiler_params=pltpu.CompilerParams(vmem_limit_bytes=1024 * 1024),
    )(out, radj)
    return out.T, radj


def solution(mesh):
    placed = (P("row", "col"), P("col", None), P("row", "col"), P("row", "col"), P("row", "col"))
    return jax.shard_map(
        local,
        mesh=mesh,
        in_specs=placed,
        out_specs=(P("row", "col"), P("row", "col")),
        check_vma=False,
    )
```

```python
import jax
import jax.numpy as jnp
from jax import lax
from jax.experimental import pallas as pl
from jax.experimental.pallas import tpu as pltpu
from jax.sharding import PartitionSpec as P

MESH = pl.DeviceIdType.MESH
f32, bf16 = jnp.float32, jnp.bfloat16
ROWS, COLS, DEPTH, KS, HALF = 1792, 448, 512, 16, 256
WIDE = ROWS + HALF
STEPS = (0, 3, 1, 2)


def split(v):
    hi = v.astype(bf16)
    return hi, (v - hi.astype(f32)).astype(bf16)


def dot(a, b, dims):
    return lax.dot_general(a, b, (dims, ((), ())), preferred_element_type=f32)


def dot3(ah, al, bh, bl, dims):
    rows = ah.shape[0]
    both = dot(jnp.concatenate([ah, al], axis=0), bh, dims)
    return both[:rows] + both[rows:] + dot(ah, bl, dims)


def kernel(
    panel, inv, rowp, adj, fac, out, radj,
    z, fbuf, fh, fl, abuf, ph, pL, dbuf, ra, tm, tp, th, tl, dth, dtl, wm, wp, wh, wl, us, ur,
    ssem, rsem, rs_s, rs_r, ts_s, ts_r, ws, us_s, us_r, loc,
):
    row, col = lax.axis_index("row"), lax.axis_index("col")
    h, core = row // 2, row % 2
    zl, x, y = col // 16, (col // 4) % 4, col % 4
    ia = x + core * (y - x)
    ib = y + core * (x - y)

    def device(zz, a, b):
        return (row, zz * 16 + a * (4 - 3 * core) + b * (1 + 3 * core))

    def off(i, d):
        return (i + d) % 4

    mate = device(1 - zl, ia, ib)
    ap, am = device(zl, off(ia, 1), ib), device(zl, off(ia, 3), ib)
    bp, bm = device(zl, ia, off(ib, 1)), device(zl, ia, off(ib, 3))
    partner = (2 * h + 1 - core, col)
    group = [(2 * ((h + d) % 4) + core, col) for d in (1, 3)]

    def plane(dz):
        return zl if dz == 0 else 1 - zl

    own = z.at[zl, ia, ib]
    l_panel = pltpu.make_async_copy(panel, own.at[:, pl.ds(0, ROWS)], loc.at[0])
    l_inv = pltpu.make_async_copy(inv, dbuf, loc.at[1])
    l_row = pltpu.make_async_copy(rowp, ra.at[h], loc.at[2])
    l_fac = pltpu.make_async_copy(fac, fbuf, loc.at[3])
    l_adj = pltpu.make_async_copy(adj, abuf, loc.at[4])
    barrier = pltpu.get_barrier_semaphore()
    others = [mate, ap, am, bp, bm, partner] + group
    for other in others:
        pl.semaphore_signal(barrier, inc=1, device_id=other, device_id_type=MESH)
    l_inv.start()
    l_panel.start()
    l_row.start()
    l_inv.wait()
    d = dbuf[...]
    even = jnp.concatenate([d[:, 128 * i : 128 * i + 64] for i in range(4)], axis=1)
    odd = jnp.concatenate([d[:, 128 * i + 64 : 128 * i + 128] for i in range(4)], axis=1)
    z[zl, ia, ib, :, ROWS:WIDE] = jnp.where(core == 0, even, odd)
    l_panel.wait()
    pl.semaphore_wait(barrier, len(others))

    sends = []

    def kind_b(dz, n, m):
        return 11 + (dz * 4 + n) * 4 + m

    def part(zz, a, b, half):
        ref = z.at[zz, a, b]
        return ref if half is None else ref.at[pl.ds(8 * half if isinstance(half, int) else pl.multiple_of(8 * half, 8), 8)]

    wa, wb = 1 - jnp.minimum(ia, 1), 1 - jnp.minimum(ib, 1)

    def side(plus, minus, m):
        return tuple(p + m * (q - p) for p, q in zip(plus, minus))

    def send(kind, ref, target):
        copy = pltpu.make_async_remote_copy(
            src_ref=ref, dst_ref=ref, send_sem=ssem.at[kind], recv_sem=rsem.at[kind],
            device_id=target, device_id_type=MESH,
        )
        copy.start()
        sends.append(copy)
        return copy

    def arrive(kind, ref):
        pltpu.make_async_remote_copy(
            src_ref=ref, dst_ref=ref, send_sem=ssem.at[kind], recv_sem=rsem.at[kind],
            device_id=mate, device_id_type=MESH,
        ).wait_recv()

    def line(dz, n):
        return part(plane(dz), off(ia, STEPS[n]), ib, None)

    def send_b(dz, n):
        send(kind_b(dz, n, 0), line(dz, n), bp)
        send(kind_b(dz, n, 1), line(dz, n), bm)

    def beside(dz, m):
        return part(plane(dz), off(ia, 3 - 2 * m), ib, None)

    def half(dz, m):
        return part(plane(dz), off(ia, 3 - 2 * m), ib, m)

    def other_half(dz, m):
        return part(plane(dz), off(ia, 3 - 2 * m), ib, 1 - m)

    def onward(m):
        return side(ap, am, m)

    def send_beside(dz, m):
        send(kind_b(dz, 1 + m, 0), beside(dz, m), bp)
        send(kind_b(dz, 1 + m, 1), beside(dz, m), bm)

    def relay_a(m):
        arrive(3 + m, beside(0, m))
        send(5 + m, half(0, m), onward(m))
        send(1 + m, other_half(0, m), mate)
        send_beside(0, m)

    def from_mate():
        arrive(0, line(1, 0))
        for m in (0, 1):
            send(7 + m, part(1 - zl, ia, ib, m), onward(m))
        send_b(1, 0)

    def relay_mate(m):
        arrive(7 + m, half(1, m))
        send(9 + m, half(1, m), onward(m))

    def from_z(m):
        arrive(1 + m, other_half(1, m))
        send_beside(1, m)

    def far_a(dz):
        for m in (0, 1):
            arrive((5 if dz == 0 else 9) + m, part(plane(dz), off(ia, 2), ib, m))
        send_b(dz, 3)

    def relay_b(dz, n):
        a = off(ia, STEPS[n])
        for m in (wb, 1 - wb):
            b = off(ib, 3 - 2 * m)
            arrive(kind_b(dz, n, m), part(plane(dz), a, b, None))
            send(kind_b(dz, n, 2 + m), part(plane(dz), a, b, m), side(bp, bm, m))

    def far_b(dz, n):
        for m in (0, 1):
            arrive(kind_b(dz, n, 2 + m), part(plane(dz), off(ia, STEPS[n]), off(ib, 2), m))

    hs = [off(h, d) for d in (0, 1, 2, 3)]
    nxt, prv = (2 * hs[1] + core, col), (2 * hs[3] + core, col)
    r_sends = []

    def r_copy(k, ref, target):
        return pltpu.make_async_remote_copy(
            src_ref=ref, dst_ref=ref, send_sem=rs_s.at[k], recv_sem=rs_r.at[k],
            device_id=target, device_id_type=MESH,
        )

    def r_send(k, ref, target):
        copy = r_copy(k, ref, target)
        copy.start()
        r_sends.append(copy)

    def r_own():
        l_row.wait()
        r_send(0, ra.at[h], nxt)
        r_send(1, ra.at[h], prv)

    def r_relay():
        r_copy(0, ra.at[hs[3]], nxt).wait_recv()
        r_send(2, ra.at[hs[3], pl.ds(0, 32)], nxt)
        r_copy(1, ra.at[hs[1]], nxt).wait_recv()
        r_send(3, ra.at[hs[1], pl.ds(32, 32)], prv)

    def r_far():
        r_copy(2, ra.at[hs[2], pl.ds(0, 32)], nxt).wait_recv()
        r_copy(3, ra.at[hs[2], pl.ds(32, 32)], nxt).wait_recv()

    def split_factor():
        l_fac.wait()
        for j in range(7):
            cut = pl.ds(256 * j, 256)
            hi, lo = split(fbuf[:, cut])
            fh[:, cut] = hi
            fl[:, cut] = lo

    t_sends = []

    def product(pieces):
        at = [(plane(dz), off(ib, STEPS[m])) for dz, m in pieces]
        v = jnp.concatenate([z[zz, :, b, :, 0:ROWS].reshape(64, ROWS) for zz, b in at], axis=0)
        hi, lo = split(v)
        for i, (zz, b) in enumerate(at):
            ph[zz, :, b] = hi[64 * i : 64 * i + 64].reshape(4, 16, ROWS)
            pL[zz, :, b] = lo[64 * i : 64 * i + 64].reshape(4, 16, ROWS)
        t = dot3(hi, lo, fh[...], fl[...], ((1,), (1,)))
        for i, (zz, b) in enumerate(at):
            tm[zz, :, b] = t[64 * i : 64 * i + 64].reshape(4, 16, COLS)
        for (dz, m), (zz, b) in zip(pieces, at):
            k = dz * 4 + m
            copy = pltpu.make_async_remote_copy(
                src_ref=tm.at[zz, :, b], dst_ref=tp.at[zz, :, b], send_sem=ts_s.at[k], recv_sem=ts_r.at[k],
                device_id=partner, device_id_type=MESH,
            )
            copy.start()
            t_sends.append(copy)

    def t_wait(dz, m):
        ref = tp.at[plane(dz), :, off(ia, STEPS[m])]
        k = dz * 4 + m
        pltpu.make_async_remote_copy(
            src_ref=ref, dst_ref=ref, send_sem=ts_s.at[k], recv_sem=ts_r.at[k],
            device_id=partner, device_id_type=MESH,
        ).wait_recv()

    def t_sum(n, m):
        a, b = off(ia, STEPS[n]), off(ib, STEPS[m])
        for zz in range(2):
            hi, lo = split(tm[zz, a, b] + tp[zz, b, a])
            th[zz, a, b] = hi
            tl[zz, a, b] = lo

    first = send(3, line(0, 0), ap)
    send(4, line(0, 0), am)
    send(0, line(0, 0), mate)
    l_fac.start()
    l_adj.start()
    first.wait_send()
    del sends[0]
    send_b(0, 0)
    relay_a(wa)
    relay_a(1 - wa)
    from_mate()
    r_own()
    relay_b(0, 0)
    split_factor()
    relay_mate(wa)
    relay_mate(1 - wa)
    far_a(0)
    from_z(0)
    from_z(1)
    relay_b(0, 1)
    relay_b(0, 2)
    far_a(1)
    relay_b(1, 0)
    relay_b(0, 3)
    product([(0, 0), (0, 1)])
    relay_b(1, 1)
    relay_b(1, 2)
    product([(0, 2), (1, 0)])
    r_relay()
    relay_b(1, 3)
    product([(1, 1), (1, 2)])
    for n in range(4):
        far_b(0, n)
    product([(0, 3)])
    for dz in (0, 1):
        for m in (0, 1, 2):
            t_wait(dz, m)
    for n in (0, 1, 2):
        for m in (0, 1, 2):
            t_sum(n, m)
    for n in range(4):
        far_b(1, n)
    product([(1, 3)])

    dh, dl = split(z[:, :, :, :, ROWS:WIDE].reshape(DEPTH, HALF))
    dth[...] = dh.T
    dtl[...] = dl.T

    t_wait(0, 3)
    t_wait(1, 3)
    for n in range(4):
        for m in range(4):
            if n == 3 or m == 3:
                t_sum(n, m)
    us[...] = dot3(
        dth[...], dtl[...], th[...].reshape(DEPTH, COLS), tl[...].reshape(DEPTH, COLS), ((1,), (0,))
    ).reshape(4, 64, COLS)
    u_sends = []

    def u_copy(k, src, target):
        return pltpu.make_async_remote_copy(
            src_ref=src, dst_ref=ur.at[k], send_sem=us_s.at[k], recv_sem=us_r.at[k],
            device_id=target, device_id_type=MESH,
        )

    def u_send(k, block, half, target):
        copy = u_copy(k, us.at[block, pl.ds(32 * half, 32)], target)
        copy.start()
        u_sends.append(copy)

    def u_arrive(k):
        u_copy(k, us.at[h, pl.ds(0, 32)], nxt).wait_recv()

    u_send(0, hs[2], 0, nxt)
    u_send(1, hs[2], 1, prv)
    u_send(2, hs[1], 1, nxt)
    u_send(3, hs[3], 0, prv)

    r_far()
    rh, rl = split(ra[...].reshape(HALF, COLS))
    wm[...] = dot3(dh, dl, rh, rl, ((1,), (0,))).reshape(2, 4, 4, 16, COLS)
    w_copy = pltpu.make_async_remote_copy(
        src_ref=wm, dst_ref=wp, send_sem=ws.at[0], recv_sem=ws.at[1], device_id=partner, device_id_type=MESH
    )
    w_copy.start()
    u_arrive(0)
    us[hs[1], 0:32] += ur[0]
    u_send(4, hs[1], 0, nxt)
    u_arrive(1)
    us[hs[3], 32:64] += ur[1]
    u_send(5, hs[3], 1, prv)
    w_copy.wait_recv()
    for zz in range(2):
        for i in range(4):
            for j in range(4):
                hi, lo = split(wm[zz, i, j] + wp[zz, j, i])
                wh[zz, i, j] = hi
                wl[zz, i, j] = lo
    l_adj.wait()
    wth = wh[...].reshape(DEPTH, COLS).T
    wtl = wl[...].reshape(DEPTH, COLS).T
    for j in range(7):
        cut = pl.ds(256 * j, 256)
        pj = ph[:, :, :, :, cut].reshape(DEPTH, 256)
        qj = pL[:, :, :, :, cut].reshape(DEPTH, 256)
        out[:, cut] = abuf[:, cut] - dot3(wth, wtl, pj, qj, ((1,), (0,)))

    for k in (2, 3, 4, 5):
        u_arrive(k)
    radj[0:32] = us[h, 0:32] + ur[4] + ur[3]
    radj[32:64] = us[h, 32:64] + ur[2] + ur[5]
    for copy in sends + r_sends + t_sends + u_sends + [w_copy]:
        copy.wait_send()


def finish(a, b, out_a, out_b, sem):
    copies = [pltpu.make_async_copy(b, out_b, sem.at[7])]
    for j in range(7):
        cut = pl.ds(64 * j, 64)
        copies.append(pltpu.make_async_copy(a.at[cut], out_a.at[cut], sem.at[j]))
    for copy in copies:
        copy.start()
    for copy in copies:
        copy.wait()


def local(panel_adj, inv_diag, row_panel, trailing_adj, trailing_factor):
    dma = pltpu.SemaphoreType.DMA
    hbm = pl.BlockSpec(memory_space=pltpu.HBM)
    v = pltpu.VMEM
    out, radj = pl.pallas_call(
        kernel,
        out_shape=(
            v((COLS, ROWS), f32),
            v((64, COLS), f32),
        ),
        in_specs=[hbm] * 5,
        out_specs=(pl.BlockSpec(memory_space=pltpu.VMEM),) * 2,
        scratch_shapes=[
            v((2, 4, 4, KS, WIDE), f32),
            v((COLS, ROWS), f32),
            v((COLS, ROWS), bf16),
            v((COLS, ROWS), bf16),
            v((COLS, ROWS), f32),
            v((2, 4, 4, KS, ROWS), bf16),
            v((2, 4, 4, KS, ROWS), bf16),
            v((KS, DEPTH), f32),
            v((4, 64, COLS), f32),
            v((2, 4, 4, KS, COLS), f32),
            v((2, 4, 4, KS, COLS), f32),
            v((2, 4, 4, KS, COLS), bf16),
            v((2, 4, 4, KS, COLS), bf16),
            v((HALF, DEPTH), bf16),
            v((HALF, DEPTH), bf16),
            v((2, 4, 4, KS, COLS), f32),
            v((2, 4, 4, KS, COLS), f32),
            v((2, 4, 4, KS, COLS), bf16),
            v((2, 4, 4, KS, COLS), bf16),
            v((4, 64, COLS), f32),
            v((6, 32, COLS), f32),
            dma((43,)),
            dma((43,)),
            dma((4,)),
            dma((4,)),
            dma((8,)),
            dma((8,)),
            dma((2,)),
            dma((6,)),
            dma((6,)),
            dma((5,)),
        ],
        compiler_params=pltpu.CompilerParams(
            collective_id=0, has_side_effects=True, vmem_limit_bytes=63_500_000
        ),
    )(panel_adj.T, inv_diag, row_panel, trailing_adj.T, trailing_factor.T)
    out, radj = pl.pallas_call(
        finish,
        out_shape=(
            jax.ShapeDtypeStruct((COLS, ROWS), f32),
            jax.ShapeDtypeStruct((64, COLS), f32),
        ),
        in_specs=[pl.BlockSpec(memory_space=pl.ANY)] * 2,
        out_specs=(hbm,) * 2,
        scratch_shapes=[dma((8,))],
        compiler_params=pltpu.CompilerParams(vmem_limit_bytes=1024 * 1024),
    )(out, radj)
    return out.T, radj


def solution(mesh):
    placed = (P("row", "col"), P("col", None), P("row", "col"), P("row", "col"), P("row", "col"))
    return jax.shard_map(
        local,
        mesh=mesh,
        in_specs=placed,
        out_specs=(P("row", "col"), P("row", "col")),
        check_vma=False,
    )
```
